32 devices in a mesh: groups: 2 (over y), patch: 8 (over z, x), heads: 2 (over core).
Axes of the slice: x: 2, y: 2, z: 4, core: 2. Of those that a mesh axis runs over, the one named last changes fastest.
Arguments:
- hidden_in: bfloat16 [512, 1280], P(('groups', 'patch'), 'heads'), parts along dimension 0, may hold values from -150 to 150
- gn_gain: float32 [1280], P('heads'), may hold values from 0.25 to 1.75
- gn_bias: float32 [1280], P('heads'), may hold values from -3 to 3
- w_in: bfloat16 [1280, 1280], P(None, 'heads'), may hold values from -0.15625 to 0.15625
- b_in: float32 [1280], P('heads'), may hold values from -3 to 3
- ln_gain: float32 [1280], replicated, may hold values from 0.25 to 1.75
- ln_bias: float32 [1280], replicated, may hold values from -3 to 3
- w_qkv: bfloat16 [3, 1280, 1280], P(None, None, 'heads'), may hold values from -0.15625 to 0.15625
- stale_kv: bfloat16 [2, 512, 1280], P(None, ('groups', 'patch'), 'heads'), parts along dimension 1, may hold values from -64 to 64
- w_out: bfloat16 [1280, 1280], P('heads'), may hold values from -0.15625 to 0.15625
- b_out: float32 [1280], P('heads'), may hold values from -3 to 3
Outputs:
- hidden_out: float32 [512, 1280], P(('groups', 'patch'), 'heads'), parts along dimension 0
The draws below stay inside these ranges and needn't reach their ends.
There are 2 independent parts, one for each index of `groups`. The reference program is written for one: setup_inputs(seed, part) draws one part's arguments, and reference() takes and returns one part's arrays. A program takes and returns all parts, laid end to end along the dimension named above; an argument that names none is the same for every part. Nothing has to cross between parts.
All inputs are finite; a program needn't handle non-finite values.
Results may differ from the reference program's by a relative error of at most 0.035.
Values may be sent and summed in bfloat16 or wider, within the bound.
No kernel may reach another device: no remote copies, remote signals or barrier semaphores. Data moves between devices by JAX's collectives and lax.ppermute only.
A program may use at most 128 MiB of HBM per device.

```python
import math
import jax
import jax.numpy as jnp
from jax import lax

C = 1280
HEADS = 20
HD = 64
GROUPS = 32
ROW_TOK = 32
TOKENS = 256
N_PATCH = 8


def draw_hidden_in(key, part):
    k_noise = jax.random.fold_in(key, 0)
    k_token = jax.random.fold_in(key, 1)
    k_chan = jax.random.fold_in(key, 2)
    k_offset = jax.random.fold_in(key, 4)
    k_osign = jax.random.fold_in(key, 5)
    noise = jnp.clip(jax.random.normal(k_noise, (TOKENS, C), jnp.float32), -4.0, 4.0)
    tok_scale = jnp.exp(jax.random.uniform(k_token, (TOKENS, GROUPS), jnp.float32, 0.0, math.log(10.0))) / 3.0
    tok_scale = jnp.repeat(tok_scale, C // GROUPS, axis=1)
    row_trend = jnp.exp(math.log(3.0) * jnp.arange(TOKENS, dtype=jnp.float32) / (TOKENS - 1)) / math.sqrt(3.0)
    chan_scale = jnp.exp(jax.random.uniform(k_chan, (C,), jnp.float32, math.log(0.4), math.log(4.0)))
    values = noise * tok_scale * row_trend[:, None] * chan_scale[None, :]
    offset_size = jax.random.uniform(k_offset, (GROUPS,), jnp.float32, 2.0, 5.0)
    offset_sign = jnp.where(jax.random.bernoulli(k_osign, 0.5, (GROUPS,)), 1.0, -1.0)
    group_offset = jnp.repeat(offset_size * offset_sign, C // GROUPS)
    position = jnp.arange(TOKENS, dtype=jnp.float32) / (TOKENS - 1)
    ramp = 0.2 + 0.8 * position
    values = values + ramp[:, None] * group_offset[None, :]
    return values.astype(jnp.bfloat16)


def draw_stale_kv(key, part):
    k_noise, k_scale = jax.random.split(key, 2)
    noise = jnp.clip(jax.random.normal(k_noise, (2, TOKENS, HEADS * HD), jnp.float32), -4.0, 4.0)
    tok_scale = jnp.exp(jax.random.uniform(k_scale, (2, TOKENS, HEADS), jnp.float32, math.log(0.5), math.log(3.0)))
    values = noise * jnp.repeat(tok_scale, HD, axis=2)
    return values.astype(jnp.bfloat16)


def block_scale(key, dims, cuts, low, largest):
    factor_of = 1.0
    for dim, parts in cuts:
        steps = jax.random.uniform(jax.random.fold_in(jax.random.fold_in(key, 6), dim), (parts,), jnp.float32, low / len(cuts), largest / len(cuts))
        factor_of = factor_of * jnp.repeat(jnp.exp(steps), dims[dim] // parts).reshape((-1,) + (1,) * (len(dims) - 1 - dim))
    return factor_of


def gaussian(stream_key, shape, width, bound, pieces=(), kind=jnp.bfloat16):
    drawn = width * jax.random.normal(stream_key, shape, jnp.float32)
    if pieces:
        drawn = drawn * block_scale(stream_key, shape, pieces, -0.22, 0.18)
    return jnp.clip(drawn, -bound, bound).astype(kind)


def setup_inputs(seed: int = 0, part: int = 0) -> dict:
    arg_keys = jax.random.split(jax.random.key(seed), 12)
    own_keys = jax.random.split(jax.random.fold_in(arg_keys[11], part), 12)
    return {
        "hidden_in": draw_hidden_in(jax.random.fold_in(jax.random.fold_in(arg_keys[11], part), 71), part),
        "gn_gain": jnp.clip(1.0 + 0.15 * jax.random.normal(arg_keys[1], (C,), jnp.float32), 0.25, 1.75),
        "gn_bias": gaussian(arg_keys[2], (C,), 0.5, 3.0, ((0, 2),), jnp.float32),
        "w_in": gaussian(arg_keys[3], (C, C), C ** -0.5, 0.15625, ((1, 2),)),
        "b_in": gaussian(arg_keys[4], (C,), 0.5, 3.0, ((0, 2),), jnp.float32),
        "ln_gain": jnp.clip(1.0 + 0.15 * jax.random.normal(arg_keys[5], (C,), jnp.float32), 0.25, 1.75),
        "ln_bias": gaussian(arg_keys[6], (C,), 0.5, 3.0, (), jnp.float32),
        "w_qkv": gaussian(arg_keys[7], (3, C, HEADS * HD), C ** -0.5, 0.15625, ((2, 2),)),
        "stale_kv": draw_stale_kv(jax.random.fold_in(jax.random.fold_in(arg_keys[11], part), 71), part),
        "w_out": gaussian(arg_keys[9], (HEADS * HD, C), (HEADS * HD) ** -0.5, 0.15625, ((0, 2),)),
        "b_out": gaussian(arg_keys[10], (C,), 0.5, 3.0, ((0, 2),), jnp.float32),
    }


def to_float(array):
    return lax.optimization_barrier(array).astype(jnp.float32)

def reference(hidden_in, gn_gain, gn_bias, w_in, b_in, ln_gain, ln_bias, w_qkv, stale_kv, w_out, b_out):
    group_size = C // GROUPS
    values = hidden_in.astype(jnp.float32).reshape(TOKENS, GROUPS, group_size)
    grp_mean = lax.optimization_barrier(jnp.mean(values, axis=(0, 2)))
    centered = values - grp_mean[None, :, None]
    grp_var = lax.optimization_barrier(jnp.mean(centered * centered, axis=(0, 2)))
    normed = (centered * lax.rsqrt(grp_var + 1e-06)[None, :, None]).reshape(TOKENS, C) * gn_gain + gn_bias
    normed = normed.astype(jnp.bfloat16)
    stream = (jnp.dot(normed, w_in, preferred_element_type=jnp.float32) + b_in).astype(jnp.bfloat16)
    stream_float = stream.astype(jnp.float32)
    tok_mean = lax.optimization_barrier(jnp.mean(stream_float, axis=1, keepdims=True))
    tok_centered = stream_float - tok_mean
    tok_var = lax.optimization_barrier(jnp.mean(tok_centered * tok_centered, axis=1, keepdims=True))
    layer_normed = (tok_centered * lax.rsqrt(tok_var + 1e-05) * ln_gain + ln_bias).astype(jnp.bfloat16)
    projections = jnp.einsum('tc,icd->itd', to_float(layer_normed), w_qkv.astype(jnp.float32)).astype(jnp.bfloat16)
    projections = to_float(projections)
    all_query = projections[0].reshape(N_PATCH, ROW_TOK, HEADS, HD)
    all_key = projections[1].reshape(N_PATCH, ROW_TOK, HEADS, HD)
    all_val = projections[2].reshape(N_PATCH, ROW_TOK, HEADS, HD)
    stale_keys = stale_kv[0].astype(jnp.float32).reshape(TOKENS, HEADS, HD)
    stale_vals = stale_kv[1].astype(jnp.float32).reshape(TOKENS, HEADS, HD)

    def attend_strip(strip_args):
        strip_idx, strip_query, strip_key, strip_val = strip_args
        first_row = (strip_idx * ROW_TOK).astype(jnp.int32)
        zero_idx = jnp.zeros((), jnp.int32)
        key_rows = lax.dynamic_update_slice(stale_keys, strip_key, (first_row, zero_idx, zero_idx))
        val_rows = lax.dynamic_update_slice(stale_vals, strip_val, (first_row, zero_idx, zero_idx))
        scores = jnp.einsum('whd,thd->wht', strip_query, key_rows) * HD ** (-0.5)
        row_max = lax.optimization_barrier(jnp.max(scores, axis=-1, keepdims=True))
        weights = jnp.exp(scores - row_max)
        weight_sum = lax.optimization_barrier(jnp.sum(weights, axis=-1))
        out_sum = jnp.einsum('wht,thd->whd', to_float(weights.astype(jnp.bfloat16)), val_rows)
        return (out_sum / weight_sum[..., None]).astype(jnp.bfloat16)
    attended = lax.map(attend_strip, (jnp.arange(N_PATCH, dtype=jnp.int32), all_query, all_key, all_val))
    attended = attended.reshape(TOKENS, HEADS * HD)
    head_terms = jnp.dot(attended, w_out, preferred_element_type=jnp.float32) + b_out
    return stream_float + head_terms
```

```python
import functools

import jax
import jax.numpy as jnp
from jax import lax
from jax.experimental import pallas as pl
from jax.experimental.pallas import tpu as pltpu
from jax.sharding import PartitionSpec as P

HD = 64
GROUPS = 32
STAT_ROWS = 16
COVER = 10_000_000_000
VMEM = pltpu.VMEM
BF = jnp.bfloat16
F32 = jnp.float32


def call(kernel, out_shape, n_in, scratch=(), spaces=None, flops=0, name=None, extra=0):
    return pl.pallas_call(
        kernel,
        out_shape=out_shape,
        in_specs=[pl.BlockSpec(memory_space=(spaces or {}).get(i, VMEM)) for i in range(n_in)],
        out_specs=jax.tree.map(lambda _: pl.BlockSpec(memory_space=VMEM), out_shape),
        scratch_shapes=list(scratch),
        cost_estimate=pl.CostEstimate(flops=flops, bytes_accessed=1 << 17, transcendentals=0),
        compiler_params=pltpu.CompilerParams(vmem_limit_bytes=(8 << 20) + extra),
        name=name,
    )


def sds(shape, dtype):
    return jax.ShapeDtypeStruct(shape, dtype)


def split3(x):
    hi = x.astype(BF)
    rest = x - hi.astype(F32)
    mid = rest.astype(BF)
    lo = (rest - mid.astype(F32)).astype(BF)
    return [hi.astype(F32), mid.astype(F32), lo.astype(F32)]


def col_stats(x):
    mean = jnp.mean(x, axis=0, keepdims=True)
    cen = x - mean
    return mean, jnp.sum(cen * cen, axis=0, keepdims=True)


def stats_kernel(own_ref, other_ref, kv_ref, msg_ref):
    tok = own_ref.shape[0]
    width = own_ref.shape[1]
    msg_ref[0:tok, :] = kv_ref[0]
    msg_ref[tok : 2 * tok, :] = kv_ref[1]
    rows = []
    for ref in (own_ref, other_ref):
        mean, m2 = col_stats(ref[...].astype(F32))
        rows += split3(mean) + split3(m2)
    rows.append(jnp.zeros((STAT_ROWS - len(rows), width), F32))
    msg_ref[2 * tok :, :] = jnp.concatenate(rows, axis=0).astype(BF)


def read_stats(msg_ref, base):
    s = msg_ref[base : base + STAT_ROWS, :].astype(F32)
    parts = [s[3 * i : 3 * i + 1] + s[3 * i + 1 : 3 * i + 2] + s[3 * i + 2 : 3 * i + 3] for i in range(4)]
    return parts


def merge_stats(parts, count):
    mean = parts[0][0]
    for p in parts[1:]:
        mean = mean + p[0]
    mean = mean * (1.0 / len(parts))
    m2 = None
    for p in parts:
        dev = p[0] - mean
        term = p[1] + count * (dev * dev)
        m2 = term if m2 is None else m2 + term
    return mean, m2


def merge_kernel(tok, *refs):
    msgs, (stat_ref, kv_ref) = refs[:-2], refs[-2:]
    all_parts = [read_stats(m, 2 * tok) for m in msgs]
    out = []
    for half in (0, 1):
        out += list(merge_stats([(p[2 * half], p[2 * half + 1]) for p in all_parts], float(tok)))
    out.append(jnp.zeros((8 - len(out), out[0].shape[1]), F32))
    stat_ref[...] = jnp.concatenate(out, axis=0)
    for i, m in enumerate(msgs[1:]):
        kv_ref[2 * tok * i : 2 * tok * (i + 1), :] = m[0 : 2 * tok, :]


def in_kernel(count, group_size, h_ref, st_a, st_b, own_ref, other_ref, gb_ref, gb2_ref, b_ref, w_ref, out_ref):
    width = own_ref.shape[1]
    n_groups = width // group_size
    a, b = st_a[...], st_b[...]
    chan = lax.broadcasted_iota(jnp.int32, (n_groups, width), 1)
    grp = lax.broadcasted_iota(jnp.int32, (n_groups, width), 0) * group_size
    hot = jnp.where((chan >= grp) & (chan < grp + group_size), 1.0, 0.0)

    def over_group(row):
        per = jnp.sum(hot * row, axis=1, keepdims=True)
        return jnp.sum(hot * per, axis=0, keepdims=True)

    h = h_ref[0]
    acc = b_ref[...]
    for half, (x_ref, g_ref) in enumerate(((own_ref, gb_ref), (other_ref, gb2_ref))):
        mean, m2 = merge_stats(
            [(a[2 * half : 2 * half + 1], a[2 * half + 1 : 2 * half + 2]), (b[2 * half : 2 * half + 1], b[2 * half + 1 : 2 * half + 2])],
            count,
        )
        g_mean = over_group(mean) * (1.0 / group_size)
        dev = mean - g_mean
        var = over_group(m2 + (2.0 * count) * (dev * dev)) * (1.0 / (2.0 * count * group_size))
        scale = lax.rsqrt(var + 1e-06) * g_ref[0:1, :]
        normed = ((x_ref[...].astype(F32) - g_mean) * scale + g_ref[1:2, :]).astype(BF)
        first = pl.multiple_of((h if half == 0 else 1 - h) * width, 128)
        acc = acc + jnp.dot(normed, w_ref[pl.ds(first, width), :], preferred_element_type=F32)
    out_ref[...] = acc.astype(BF)


def qkv_kernel(h_ref, own_ref, other_ref, ln_ref, w_ref, out_ref):
    tok, width = own_ref.shape
    full = 2 * width
    x = [own_ref[...].astype(F32), other_ref[...].astype(F32)]
    mean = (jnp.sum(x[0], axis=1, keepdims=True) + jnp.sum(x[1], axis=1, keepdims=True)) / full
    x = [v - mean for v in x]
    var = (jnp.sum(x[0] * x[0], axis=1, keepdims=True) + jnp.sum(x[1] * x[1], axis=1, keepdims=True)) / full
    rstd = lax.rsqrt(var + 1e-05)
    h = h_ref[0]
    firsts = [pl.multiple_of(h * width, 128), pl.multiple_of((1 - h) * width, 128)]
    normed = [
        (v * rstd * ln_ref[0:1, pl.ds(f, width)] + ln_ref[1:2, pl.ds(f, width)]).astype(BF) for v, f in zip(x, firsts)
    ]
    for i in range(3):
        acc = jnp.dot(normed[0], w_ref[i, pl.ds(firsts[0], width), :], preferred_element_type=F32)
        acc = acc + jnp.dot(normed[1], w_ref[i, pl.ds(firsts[1], width), :], preferred_element_type=F32)
        out_ref[i] = acc.astype(BF)


def attn_kernel(sources, h_ref, qkv_ref, *refs):
    n_src = max((s[0] for s in sources), default=-1) + 1
    srcs, w_ref, att_ref, send_ref, k_scr, v_scr = refs[:n_src], *refs[n_src:]
    tok, width = qkv_ref.shape[1:]
    at = 0
    if len(srcs) == 0 or sources[0][4]:
        k_scr[0:tok, :] = qkv_ref[1]
        v_scr[0:tok, :] = qkv_ref[2]
        at = tok
    for i, k0, v0, rows, _ in sources:
        k_scr[at : at + rows, :] = srcs[i][k0 : k0 + rows, :]
        v_scr[at : at + rows, :] = srcs[i][v0 : v0 + rows, :]
        at += rows
    pair = 2 * HD
    low = lax.broadcasted_iota(jnp.int32, (tok, pair), 1) < HD
    for p in range(width // pair):
        cols = slice(p * pair, (p + 1) * pair)
        q = qkv_ref[0, :, cols].astype(F32) * (HD ** (-0.5))
        q2 = jnp.concatenate([jnp.where(low, q, 0.0), jnp.where(low, 0.0, q)], axis=0).astype(BF)
        scores = lax.dot_general(q2, k_scr[:, cols], (((1,), (1,)), ((), ())), preferred_element_type=F32)
        top = jnp.max(scores, axis=1, keepdims=True)
        wts = jnp.exp(scores - top)
        total = jnp.sum(wts, axis=1, keepdims=True)
        out = jnp.dot(wts.astype(BF), v_scr[:, cols], preferred_element_type=F32) / total
        att_ref[:, cols] = jnp.where(low, out[0:tok], out[tok:]).astype(BF)
    first = pl.multiple_of((1 - h_ref[0]) * width, 128)
    send_ref[...] = jnp.dot(att_ref[...], w_ref[:, pl.ds(first, width)], preferred_element_type=F32)


def own_kernel(h_ref, att_ref, stream_ref, b_ref, w_ref, out_ref):
    width = stream_ref.shape[1]
    first = pl.multiple_of(h_ref[0] * width, 128)
    part = jnp.dot(att_ref[...], w_ref[:, pl.ds(first, width)], preferred_element_type=F32)
    out_ref[...] = part + stream_ref[...].astype(F32) + b_ref[...]


def body(hidden_in, gn_gain, gn_bias, w_in, b_in, ln_gain, ln_bias, w_qkv, stale_kv, w_out, b_out):
    tok, width = hidden_in.shape
    full = ln_gain.shape[0]
    group_size = full // GROUPS
    n = lax.axis_size("patch")
    swap = [(0, 1), (1, 0)]
    h = lax.axis_index("heads").astype(jnp.int32).reshape(1)
    smem = {0: pltpu.SMEM}

    other = lax.ppermute(hidden_in, "heads", swap)
    gb = jnp.stack([gn_gain, gn_bias])
    gb_other = lax.ppermute(gb, "heads", swap)
    ln = jnp.stack([ln_gain, ln_bias])

    msg_rows = 2 * tok + STAT_ROWS
    msg = call(stats_kernel, sds((msg_rows, width), BF), 3, name="stats", flops=COVER)(hidden_in, other, stale_kv)
    partner = lambda k: [(i, i ^ k) for i in range(n)]
    stat_out = sds((8, width), F32)
    if n == 8:
        z = [lax.ppermute(msg, "patch", partner(k)) for k in (4, 6, 2)]
        x_own = lax.ppermute(msg, "patch", partner(1))
        stat, kv3 = call(
            functools.partial(merge_kernel, tok), (stat_out, sds((3 * 2 * tok, width), BF)), 4, name="merge", flops=COVER
        )(msg, *z)
        stat_x = lax.ppermute(stat, "patch", partner(1))
        x_three = lax.ppermute(kv3, "patch", partner(1))
        count = float(tok * (n // 2))
        strips = [x_own, kv3, x_three]
        sources = [(0, 0, tok, tok, True)]
        for i in (1, 2):
            sources += [(i, 2 * tok * j, 2 * tok * j + tok, tok, True) for j in range(3)]
        n_keys = n * tok
    else:
        rows = lax.all_gather(msg[2 * tok :], "patch").astype(F32)
        rows = rows[:, :12].reshape(n, 4, 3, width).sum(axis=2)
        means, m2s = rows[:, 0::2], rows[:, 1::2]
        mean = means.mean(axis=0)
        m2 = m2s.sum(axis=0) + float(tok) * ((means - mean[None]) ** 2).sum(axis=0)
        stat = jnp.concatenate([jnp.stack([mean[0], 0.5 * m2[0], mean[1], 0.5 * m2[1]]), jnp.zeros((4, width), F32)])
        stat_x = stat
        count = float(tok * n) / 2.0

    stream = call(
        functools.partial(in_kernel, count, group_size), sds((tok, width), BF), 9, spaces=smem, name="inproj", flops=COVER
    )(h, stat, stat_x, hidden_in, other, gb, gb_other, b_in.reshape(1, width), w_in)
    stream_other = lax.ppermute(stream, "heads", swap)
    qkv = call(qkv_kernel, sds((3, tok, width), BF), 5, spaces=smem, name="qkv", flops=COVER)(h, stream, stream_other, ln, w_qkv)
    if n != 8:
        kv_all = lax.all_gather(stale_kv, "patch", axis=1, tiled=True)
        kv_all = lax.dynamic_update_slice(kv_all, qkv[1:], (0, lax.axis_index("patch") * tok, 0))
        n_keys = n * tok
        strips = [kv_all.reshape(2 * n_keys, width)]
        sources = [(0, 0, n_keys, n_keys, False)]
    attended, send = call(
        functools.partial(attn_kernel, sources),
        (sds((tok, width), BF), sds((tok, width), F32)),
        3 + len(strips),
        scratch=[VMEM((n_keys, width), BF), VMEM((n_keys, width), BF)],
        extra=4 * n_keys * width + 16 * 2 * tok * n_keys,
        spaces=smem,
        name="attn",
    )(h, qkv, *strips, w_out)
    received = lax.ppermute(send, "heads", swap)
    mine = call(own_kernel, sds((tok, width), F32), 5, spaces=smem, name="own")(
        h, attended, stream, b_out.reshape(1, width), w_out
    )
    return mine + received


def solution(mesh):
    placed = (
        P(("groups", "patch"), "heads"),
        P("heads"),
        P("heads"),
        P(None, "heads"),
        P("heads"),
        P(),
        P(),
        P(None, None, "heads"),
        P(None, ("groups", "patch"), "heads"),
        P("heads", None),
        P("heads"),
    )
    return jax.shard_map(
        body, mesh=mesh, in_specs=placed, out_specs=P(("groups", "patch"), "heads"), check_vma=False
    )
```

```python
import functools

import jax
import jax.numpy as jnp
from jax import lax
from jax.experimental import pallas as pl
from jax.experimental.pallas import tpu as pltpu
from jax.sharding import PartitionSpec as P


HD = 64
GROUPS = 32
STAT_ROWS = 16
COVER = 10_000_000_000
VMEM = pltpu.VMEM
BF = jnp.bfloat16
F32 = jnp.float32


def call(kernel, out_shape, n_in, scratch=(), spaces=None, flops=0, extra=0):
    return pl.pallas_call(
        kernel,
        out_shape=out_shape,
        in_specs=[pl.BlockSpec(memory_space=(spaces or {}).get(i, VMEM)) for i in range(n_in)],
        out_specs=jax.tree.map(lambda _: pl.BlockSpec(memory_space=VMEM), out_shape),
        scratch_shapes=list(scratch),
        cost_estimate=pl.CostEstimate(flops=flops, bytes_accessed=1 << 17, transcendentals=0),
        compiler_params=pltpu.CompilerParams(vmem_limit_bytes=(8 << 20) + extra),
    )


def sds(shape, dtype):
    return jax.ShapeDtypeStruct(shape, dtype)


def split3(x):
    hi = x.astype(BF)
    rest = x - hi.astype(F32)
    mid = rest.astype(BF)
    lo = (rest - mid.astype(F32)).astype(BF)
    return [hi.astype(F32), mid.astype(F32), lo.astype(F32)]


def col_stats(x):
    mean = jnp.mean(x, axis=0, keepdims=True)
    cen = x - mean
    return mean, jnp.sum(cen * cen, axis=0, keepdims=True)


def tick_kernel(out_ref):
    out_ref[...] = jnp.zeros_like(out_ref)


def stats_kernel(own_ref, other_ref, kv_ref, gain_ref, bias_ref, tick_ref, msg_ref, gb_ref):
    tok, width = own_ref.shape
    msg_ref[0 : 2 * tok, :] = kv_ref[...]
    rows = []
    for ref in (own_ref, other_ref):
        mean, m2 = col_stats(ref[...].astype(F32))
        rows += split3(mean) + split3(m2)
    rows.append(jnp.zeros((STAT_ROWS - len(rows), width), F32))
    msg_ref[2 * tok :, :] = jnp.concatenate(rows, axis=0).astype(BF)
    gb_ref[0:1, :] = gain_ref[...].reshape(1, width)
    gb_ref[1:2, :] = bias_ref[...].reshape(1, width)


def read_stats(msg_ref, base):
    s = msg_ref[base : base + STAT_ROWS, :].astype(F32)
    parts = [s[3 * i : 3 * i + 1] + s[3 * i + 1 : 3 * i + 2] + s[3 * i + 2 : 3 * i + 3] for i in range(4)]
    return parts


def merge_stats(parts, count):
    mean = parts[0][0]
    for p in parts[1:]:
        mean = mean + p[0]
    mean = mean * (1.0 / len(parts))
    m2 = None
    for p in parts:
        dev = p[0] - mean
        term = p[1] + count * (dev * dev)
        m2 = term if m2 is None else m2 + term
    return mean, m2


def merge_kernel(tok, *refs):
    msgs, (stat_ref, kv_ref) = refs[:-2], refs[-2:]
    all_parts = [read_stats(m, 2 * tok) for m in msgs]
    out = []
    for half in (0, 1):
        out += list(merge_stats([(p[2 * half], p[2 * half + 1]) for p in all_parts], float(tok)))
    out.append(jnp.zeros((8 - len(out), out[0].shape[1]), F32))
    stat_ref[...] = jnp.concatenate(out, axis=0)
    for i, m in enumerate(msgs[1:3]):
        kv_ref[2 * tok * i : 2 * tok * (i + 1), :] = m[0 : 2 * tok, :]


def in_kernel(count, group_size, h_ref, st_a, st_b, own_ref, other_ref, gb_ref, gb2_ref, b_ref, w_ref, out_ref):
    width = own_ref.shape[1]
    n_groups = width // group_size
    a, b = st_a[...], st_b[...]
    chan = lax.broadcasted_iota(jnp.int32, (n_groups, width), 1)
    grp = lax.broadcasted_iota(jnp.int32, (n_groups, width), 0) * group_size
    hot = jnp.where((chan >= grp) & (chan < grp + group_size), 1.0, 0.0)

    def over_group(row):
        per = jnp.sum(hot * row, axis=1, keepdims=True)
        return jnp.sum(hot * per, axis=0, keepdims=True)

    h = h_ref[0]
    acc = b_ref[...].reshape(1, width)
    for half, (x_ref, g_ref) in enumerate(((own_ref, gb_ref), (other_ref, gb2_ref))):
        mean, m2 = merge_stats(
            [(a[2 * half : 2 * half + 1], a[2 * half + 1 : 2 * half + 2]), (b[2 * half : 2 * half + 1], b[2 * half + 1 : 2 * half + 2])],
            count,
        )
        g_mean = over_group(mean) * (1.0 / group_size)
        dev = mean - g_mean
        var = over_group(m2 + (2.0 * count) * (dev * dev)) * (1.0 / (2.0 * count * group_size))
        scale = lax.rsqrt(var + 1e-06) * g_ref[0:1, :]
        normed = ((x_ref[...].astype(F32) - g_mean) * scale + g_ref[1:2, :]).astype(BF)
        first = pl.multiple_of((h if half == 0 else 1 - h) * width, 128)
        acc = acc + jnp.dot(normed, w_ref[pl.ds(first, width), :], preferred_element_type=F32)
    out_ref[...] = acc.astype(BF)


def qkv_kernel(h_ref, own_ref, other_ref, gain_ref, bias_ref, w_ref, out_ref):
    _, width = own_ref.shape
    full = 2 * width
    x = [own_ref[...].astype(F32), other_ref[...].astype(F32)]
    mean = (jnp.sum(x[0], axis=1, keepdims=True) + jnp.sum(x[1], axis=1, keepdims=True)) / full
    x = [v - mean for v in x]
    var = (jnp.sum(x[0] * x[0], axis=1, keepdims=True) + jnp.sum(x[1] * x[1], axis=1, keepdims=True)) / full
    rstd = lax.rsqrt(var + 1e-05)
    h = h_ref[0]
    firsts = [pl.multiple_of(h * width, 128), pl.multiple_of((1 - h) * width, 128)]
    gain, bias = ([r[pl.ds(f, width)].reshape(1, width) for f in firsts] for r in (gain_ref, bias_ref))
    normed = [(v * rstd * g + b).astype(BF) for v, g, b in zip(x, gain, bias)]
    for i in range(3):
        acc = jnp.dot(normed[0], w_ref[i, pl.ds(firsts[0], width), :], preferred_element_type=F32)
        acc = acc + jnp.dot(normed[1], w_ref[i, pl.ds(firsts[1], width), :], preferred_element_type=F32)
        out_ref[i] = acc.astype(BF)


def attn_kernel(sources, h_ref, qkv_ref, *refs):
    n_src = max((s[0] for s in sources), default=-1) + 1
    srcs, w_ref, att_ref, send_ref, k_scr, v_scr = refs[:n_src], *refs[n_src:]
    tok, width = qkv_ref.shape[1:]
    at = 0
    if len(srcs) == 0 or sources[0][4]:
        k_scr[0:tok, :] = qkv_ref[1]
        v_scr[0:tok, :] = qkv_ref[2]
        at = tok
    for i, k0, v0, rows, _ in sources:
        k_scr[at : at + rows, :] = srcs[i][k0 : k0 + rows, :]
        v_scr[at : at + rows, :] = srcs[i][v0 : v0 + rows, :]
        at += rows
    pair = 2 * HD
    low = lax.broadcasted_iota(jnp.int32, (tok, pair), 1) < HD
    for p in range(width // pair):
        cols = slice(p * pair, (p + 1) * pair)
        q = qkv_ref[0, :, cols].astype(F32) * (HD ** (-0.5))
        q2 = jnp.concatenate([jnp.where(low, q, 0.0), jnp.where(low, 0.0, q)], axis=0).astype(BF)
        scores = lax.dot_general(q2, k_scr[:, cols], (((1,), (1,)), ((), ())), preferred_element_type=F32)
        top = jnp.max(scores, axis=1, keepdims=True)
        wts = jnp.exp(scores - top)
        total = jnp.sum(wts, axis=1, keepdims=True)
        out = jnp.dot(wts.astype(BF), v_scr[:, cols], preferred_element_type=F32) / total
        att_ref[:, cols] = jnp.where(low, out[0:tok], out[tok:]).astype(BF)
    first = pl.multiple_of((1 - h_ref[0]) * width, 128)
    send_ref[...] = jnp.dot(att_ref[...], w_ref[:, pl.ds(first, width)], preferred_element_type=F32)


def own_kernel(h_ref, att_ref, stream_ref, b_ref, w_ref, out_ref):
    width = stream_ref.shape[1]
    first = pl.multiple_of(h_ref[0] * width, 128)
    part = jnp.dot(att_ref[...], w_ref[:, pl.ds(first, width)], preferred_element_type=F32)
    out_ref[...] = part + stream_ref[...].astype(F32) + b_ref[...].reshape(1, width)


def body(hidden_in, gn_gain, gn_bias, w_in, b_in, ln_gain, ln_bias, w_qkv, stale_kv, w_out, b_out):
    tok, width = hidden_in.shape
    full = ln_gain.shape[0]
    group_size = full // GROUPS
    n = lax.axis_size("patch")
    swap = [(0, 1), (1, 0)]
    h = lax.axis_index("heads").astype(jnp.int32).reshape(1)
    smem = {0: pltpu.SMEM}

    kv_own = stale_kv.reshape(2 * tok, width)
    partner = lambda k: [(i, i ^ k) for i in range(n)]

    def move(x, k):
        return lax.ppermute(x, "patch", partner(k)) if k else lax.ppermute(x, "heads", swap)

    direct = n == 8
    if direct:
        strip_x = move(kv_own, 1)
    other = move(hidden_in, 0)
    tick = call(tick_kernel, sds((8, 128), F32), 0, flops=COVER)()
    msg, gb = call(
        stats_kernel, (sds((2 * tok + STAT_ROWS, width), BF), sds((2, width), F32)), 6, flops=COVER
    )(hidden_in, other, kv_own, gn_gain, gn_bias, tick)
    stat_out = sds((8, width), F32)
    if direct:
        z2, z3, z1 = move(msg, 4), move(msg, 6), move(msg, 2)
        strip_xz1 = move(kv_own, 3)
        gb_other = move(gb, 0)
        stat, kv2 = call(
            functools.partial(merge_kernel, tok), (stat_out, sds((2 * 2 * tok, width), BF)), 4, flops=COVER
        )(msg, z2, z3, z1)
        stat_x = move(stat, 1)
        strip_two = move(kv2, 1)
        count = float(tok * (n // 2))
        strips = [strip_x, z1, strip_xz1, kv2, strip_two]
        sources = [(i, 0, tok, tok, True) for i in range(3)]
        for i in (3, 4):
            sources += [(i, 2 * tok * j, 2 * tok * j + tok, tok, True) for j in range(2)]
    else:
        gb_other = move(gb, 0)
        rows = lax.all_gather(msg[2 * tok :], "patch").astype(F32)
        rows = rows[:, :12].reshape(n, 4, 3, width).sum(axis=2)
        means, m2s = rows[:, 0::2], rows[:, 1::2]
        mean = means.mean(axis=0)
        m2 = m2s.sum(axis=0) + float(tok) * ((means - mean[None]) ** 2).sum(axis=0)
        stat = jnp.concatenate([jnp.stack([mean[0], 0.5 * m2[0], mean[1], 0.5 * m2[1]]), jnp.zeros((4, width), F32)])
        stat_x = stat
        count = float(tok * n) / 2.0

    stream = call(
        functools.partial(in_kernel, count, group_size), sds((tok, width), BF), 9, spaces=smem, flops=COVER
    )(h, stat, stat_x, hidden_in, other, gb, gb_other, b_in, w_in)
    stream_other = move(stream, 0)
    qkv = call(qkv_kernel, sds((3, tok, width), BF), 6, spaces=smem, flops=COVER)(
        h, stream, stream_other, ln_gain, ln_bias, w_qkv
    )
    n_keys = n * tok
    if not direct:
        kv_all = lax.all_gather(stale_kv, "patch", axis=1, tiled=True)
        kv_all = lax.dynamic_update_slice(kv_all, qkv[1:], (0, lax.axis_index("patch") * tok, 0))
        strips = [kv_all.reshape(2 * n_keys, width)]
        sources = [(0, 0, n_keys, n_keys, False)]
    attended, send = call(
        functools.partial(attn_kernel, sources),
        (sds((tok, width), BF), sds((tok, width), F32)),
        3 + len(strips),
        scratch=[VMEM((n_keys, width), BF), VMEM((n_keys, width), BF)],
        extra=4 * n_keys * width + 16 * 2 * tok * n_keys,
        spaces=smem,
    )(h, qkv, *strips, w_out)
    received = move(send, 0)
    mine = call(own_kernel, sds((tok, width), F32), 5, spaces=smem)(h, attended, stream, b_out, w_out)
    return mine + received


def solution(mesh):
    placed = (
        P(("groups", "patch"), "heads"),
        P("heads"),
        P("heads"),
        P(None, "heads"),
        P("heads"),
        P(),
        P(),
        P(None, None, "heads"),
        P(None, ("groups", "patch"), "heads"),
        P("heads", None),
        P("heads"),
    )

    return jax.shard_map(body, mesh=mesh, in_specs=placed, out_specs=P(("groups", "patch"), "heads"), check_vma=False)
```

```python
import functools

import jax
import jax.numpy as jnp
from jax import lax
from jax.experimental import pallas as pl
from jax.experimental.pallas import tpu as pltpu
from jax.sharding import PartitionSpec as P


HD = 64
GROUPS = 32
STAT_ROWS = 16
COVER = 10_000_000_000
VMEM = pltpu.VMEM
BF = jnp.bfloat16
F32 = jnp.float32


def call(kernel, out_shape, n_in, scratch=(), spaces=None, flops=0, extra=0):
    return pl.pallas_call(
        kernel,
        out_shape=out_shape,
        in_specs=[pl.BlockSpec(memory_space=(spaces or {}).get(i, VMEM)) for i in range(n_in)],
        out_specs=jax.tree.map(lambda _: pl.BlockSpec(memory_space=VMEM), out_shape),
        scratch_shapes=list(scratch),
        cost_estimate=pl.CostEstimate(flops=flops, bytes_accessed=1 << 17, transcendentals=0),
        compiler_params=pltpu.CompilerParams(vmem_limit_bytes=(8 << 20) + extra),
    )


def sds(shape, dtype):
    return jax.ShapeDtypeStruct(shape, dtype)


def split3(x):
    hi = x.astype(BF)
    rest = x - hi.astype(F32)
    mid = rest.astype(BF)
    lo = (rest - mid.astype(F32)).astype(BF)
    return [hi.astype(F32), mid.astype(F32), lo.astype(F32)]


def col_stats(x):
    mean = jnp.mean(x, axis=0, keepdims=True)
    cen = x - mean
    return mean, jnp.sum(cen * cen, axis=0, keepdims=True)


def tick_kernel(out_ref):
    out_ref[...] = jnp.zeros_like(out_ref)


def stats_kernel(own_ref, other_ref, kv_ref, gain_ref, bias_ref, tick_ref, msg_ref, gb_ref):
    tok, width = own_ref.shape
    msg_ref[0 : 2 * tok, :] = kv_ref[...]
    rows = []
    for ref in (own_ref, other_ref):
        mean, m2 = col_stats(ref[...].astype(F32))
        rows += split3(mean) + split3(m2)
    rows.append(jnp.zeros((STAT_ROWS - len(rows), width), F32))
    msg_ref[2 * tok :, :] = jnp.concatenate(rows, axis=0).astype(BF)
    gb_ref[0:1, :] = gain_ref[...].reshape(1, width)
    gb_ref[1:2, :] = bias_ref[...].reshape(1, width)


def read_stats(msg_ref, base):
    s = msg_ref[base : base + STAT_ROWS, :].astype(F32)
    parts = [s[3 * i : 3 * i + 1] + s[3 * i + 1 : 3 * i + 2] + s[3 * i + 2 : 3 * i + 3] for i in range(4)]
    return parts


def merge_stats(parts, count):
    mean = parts[0][0]
    for p in parts[1:]:
        mean = mean + p[0]
    mean = mean * (1.0 / len(parts))
    m2 = None
    for p in parts:
        dev = p[0] - mean
        term = p[1] + count * (dev * dev)
        m2 = term if m2 is None else m2 + term
    return mean, m2


def merge_kernel(tok, *refs):
    msgs, (stat_ref, kv_ref) = refs[:-2], refs[-2:]
    all_parts = [read_stats(m, 2 * tok) for m in msgs]
    out = []
    for half in (0, 1):
        out += list(merge_stats([(p[2 * half], p[2 * half + 1]) for p in all_parts], float(tok)))
    out.append(jnp.zeros((8 - len(out), out[0].shape[1]), F32))
    stat_ref[...] = jnp.concatenate(out, axis=0)
    for i, m in enumerate(msgs[1:3]):
        kv_ref[2 * tok * i : 2 * tok * (i + 1), :] = m[0 : 2 * tok, :]


def in_kernel(count, group_size, st_a, st_b, own_ref, other_ref, gb_ref, gb2_ref, b_ref, w_ref, out_ref):
    width = own_ref.shape[1]
    n_groups = width // group_size
    a, b = st_a[...], st_b[...]
    chan = lax.broadcasted_iota(jnp.int32, (n_groups, width), 1)
    grp = lax.broadcasted_iota(jnp.int32, (n_groups, width), 0) * group_size
    hot = jnp.where((chan >= grp) & (chan < grp + group_size), 1.0, 0.0)

    def over_group(row):
        per = jnp.sum(hot * row, axis=1, keepdims=True)
        return jnp.sum(hot * per, axis=0, keepdims=True)

    h = lax.axis_index("heads")
    acc = b_ref[...].reshape(1, width)
    for half, (x_ref, g_ref) in enumerate(((own_ref, gb_ref), (other_ref, gb2_ref))):
        mean, m2 = merge_stats(
            [(a[2 * half : 2 * half + 1], a[2 * half + 1 : 2 * half + 2]), (b[2 * half : 2 * half + 1], b[2 * half + 1 : 2 * half + 2])],
            count,
        )
        g_mean = over_group(mean) * (1.0 / group_size)
        dev = mean - g_mean
        var = over_group(m2 + (2.0 * count) * (dev * dev)) * (1.0 / (2.0 * count * group_size))
        scale = lax.rsqrt(var + 1e-06) * g_ref[0:1, :]
        normed = ((x_ref[...].astype(F32) - g_mean) * scale + g_ref[1:2, :]).astype(BF)
        first = pl.multiple_of((h if half == 0 else 1 - h) * width, 128)
        acc = acc + jnp.dot(normed, w_ref[pl.ds(first, width), :], preferred_element_type=F32)
    out_ref[...] = acc.astype(BF)


def qkv_kernel(own_ref, other_ref, gain_ref, bias_ref, w_ref, out_ref):
    _, width = own_ref.shape
    full = 2 * width
    x = [own_ref[...].astype(F32), other_ref[...].astype(F32)]
    mean = (jnp.sum(x[0], axis=1, keepdims=True) + jnp.sum(x[1], axis=1, keepdims=True)) / full
    x = [v - mean for v in x]
    var = (jnp.sum(x[0] * x[0], axis=1, keepdims=True) + jnp.sum(x[1] * x[1], axis=1, keepdims=True)) / full
    rstd = lax.rsqrt(var + 1e-05)
    h = lax.axis_index("heads")
    firsts = [pl.multiple_of(h * width, 128), pl.multiple_of((1 - h) * width, 128)]
    gain, bias = ([r[pl.ds(f, width)].reshape(1, width) for f in firsts] for r in (gain_ref, bias_ref))
    normed = [(v * rstd * g + b).astype(BF) for v, g, b in zip(x, gain, bias)]
    for i in range(3):
        acc = jnp.dot(normed[0], w_ref[i, pl.ds(firsts[0], width), :], preferred_element_type=F32)
        acc = acc + jnp.dot(normed[1], w_ref[i, pl.ds(firsts[1], width), :], preferred_element_type=F32)
        out_ref[i] = acc.astype(BF)


def attn_kernel(sources, qkv_ref, *refs):
    n_src = max((s[0] for s in sources), default=-1) + 1
    srcs, w_ref, att_ref, send_ref, k_scr, v_scr = refs[:n_src], *refs[n_src:]
    tok, width = qkv_ref.shape[1:]
    at = 0
    if len(srcs) == 0 or sources[0][4]:
        k_scr[0:tok, :] = qkv_ref[1]
        v_scr[0:tok, :] = qkv_ref[2]
        at = tok
    for i, k0, v0, rows, _ in sources:
        k_scr[at : at + rows, :] = srcs[i][k0 : k0 + rows, :]
        v_scr[at : at + rows, :] = srcs[i][v0 : v0 + rows, :]
        at += rows
    pair = 2 * HD
    low = lax.broadcasted_iota(jnp.int32, (tok, pair), 1) < HD
    for p in range(width // pair):
        cols = slice(p * pair, (p + 1) * pair)
        q = qkv_ref[0, :, cols].astype(F32) * (HD ** (-0.5))
        q2 = jnp.concatenate([jnp.where(low, q, 0.0), jnp.where(low, 0.0, q)], axis=0).astype(BF)
        scores = lax.dot_general(q2, k_scr[:, cols], (((1,), (1,)), ((), ())), preferred_element_type=F32)
        top = jnp.max(scores, axis=1, keepdims=True)
        wts = jnp.exp(scores - top)
        total = jnp.sum(wts, axis=1, keepdims=True)
        out = jnp.dot(wts.astype(BF), v_scr[:, cols], preferred_element_type=F32) / total
        att_ref[:, cols] = jnp.where(low, out[0:tok], out[tok:]).astype(BF)
    first = pl.multiple_of((1 - lax.axis_index("heads")) * width, 128)
    send_ref[...] = jnp.dot(att_ref[...], w_ref[:, pl.ds(first, width)], preferred_element_type=F32)


def own_kernel(att_ref, stream_ref, b_ref, w_ref, out_ref):
    width = stream_ref.shape[1]
    first = pl.multiple_of(lax.axis_index("heads") * width, 128)
    part = jnp.dot(att_ref[...], w_ref[:, pl.ds(first, width)], preferred_element_type=F32)
    out_ref[...] = part + stream_ref[...].astype(F32) + b_ref[...].reshape(1, width)


def body(hidden_in, gn_gain, gn_bias, w_in, b_in, ln_gain, ln_bias, w_qkv, stale_kv, w_out, b_out):
    tok, width = hidden_in.shape
    full = ln_gain.shape[0]
    group_size = full // GROUPS
    n = lax.axis_size("patch")
    swap = [(0, 1), (1, 0)]

    kv_own = stale_kv.reshape(2 * tok, width)
    partner = lambda k: [(i, i ^ k) for i in range(n)]

    def move(x, k):
        return lax.ppermute(x, "patch", partner(k)) if k else lax.ppermute(x, "heads", swap)

    direct = n == 8
    if direct:
        strip_x = move(kv_own, 1)
    other = move(hidden_in, 0)
    tick = call(tick_kernel, sds((8, 128), F32), 0, flops=COVER)()
    msg, gb = call(
        stats_kernel, (sds((2 * tok + STAT_ROWS, width), BF), sds((2, width), F32)), 6, flops=COVER
    )(hidden_in, other, kv_own, gn_gain, gn_bias, tick)
    stat_out = sds((8, width), F32)
    if direct:
        z2, z3, z1 = move(msg, 4), move(msg, 6), move(msg, 2)
        strip_xz1 = move(kv_own, 3)
        gb_other = move(gb, 0)
        stat, kv2 = call(
            functools.partial(merge_kernel, tok), (stat_out, sds((2 * 2 * tok, width), BF)), 4, flops=COVER
        )(msg, z2, z3, z1)
        stat_x = move(stat, 1)
        strip_two = move(kv2, 1)
        count = float(tok * (n // 2))
        strips = [strip_x, z1, strip_xz1, kv2, strip_two]
        sources = [(i, 0, tok, tok, True) for i in range(3)]
        for i in (3, 4):
            sources += [(i, 2 * tok * j, 2 * tok * j + tok, tok, True) for j in range(2)]
    else:
        gb_other = move(gb, 0)
        rows = lax.all_gather(msg[2 * tok :], "patch").astype(F32)
        rows = rows[:, :12].reshape(n, 4, 3, width).sum(axis=2)
        means, m2s = rows[:, 0::2], rows[:, 1::2]
        mean = means.mean(axis=0)
        m2 = m2s.sum(axis=0) + float(tok) * ((means - mean[None]) ** 2).sum(axis=0)
        stat = jnp.concatenate([jnp.stack([mean[0], 0.5 * m2[0], mean[1], 0.5 * m2[1]]), jnp.zeros((4, width), F32)])
        stat_x = stat
        count = float(tok * n) / 2.0

    stream = call(
        functools.partial(in_kernel, count, group_size), sds((tok, width), BF), 8, flops=COVER
    )(stat, stat_x, hidden_in, other, gb, gb_other, b_in, w_in)
    stream_other = move(stream, 0)
    qkv = call(qkv_kernel, sds((3, tok, width), BF), 5, flops=COVER)(stream, stream_other, ln_gain, ln_bias, w_qkv)
    n_keys = n * tok
    if not direct:
        kv_all = lax.all_gather(stale_kv, "patch", axis=1, tiled=True)
        kv_all = lax.dynamic_update_slice(kv_all, qkv[1:], (0, lax.axis_index("patch") * tok, 0))
        strips = [kv_all.reshape(2 * n_keys, width)]
        sources = [(0, 0, n_keys, n_keys, False)]
    attended, send = call(
        functools.partial(attn_kernel, sources),
        (sds((tok, width), BF), sds((tok, width), F32)),
        2 + len(strips),
        scratch=[VMEM((n_keys, width), BF), VMEM((n_keys, width), BF)],
        extra=4 * n_keys * width + 16 * 2 * tok * n_keys,
    )(qkv, *strips, w_out)
    received = move(send, 0)
    mine = call(own_kernel, sds((tok, width), F32), 4)(attended, stream, b_out, w_out)
    return mine + received


def solution(mesh):
    placed = (
        P(("groups", "patch"), "heads"),
        P("heads"),
        P("heads"),
        P(None, "heads"),
        P("heads"),
        P(),
        P(),
        P(None, None, "heads"),
        P(None, ("groups", "patch"), "heads"),
        P("heads", None),
        P("heads"),
    )

    return jax.shard_map(body, mesh=mesh, in_specs=placed, out_specs=P(("groups", "patch"), "heads"), check_vma=False)
```

```python
import functools

import jax
import jax.numpy as jnp
from jax import lax
from jax.experimental import pallas as pl
from jax.experimental.pallas import tpu as pltpu
from jax.sharding import PartitionSpec as P


HD = 64
GROUPS = 32
STAT_ROWS = 4
COVER = 10_000_000_000
VMEM = pltpu.VMEM
BF = jnp.bfloat16
F32 = jnp.float32


def call(kernel, out_shape, n_in, scratch=(), spaces=None, flops=0, extra=0):
    return pl.pallas_call(
        kernel,
        out_shape=out_shape,
        in_specs=[pl.BlockSpec(memory_space=(spaces or {}).get(i, VMEM)) for i in range(n_in)],
        out_specs=jax.tree.map(lambda _: pl.BlockSpec(memory_space=VMEM), out_shape),
        scratch_shapes=list(scratch),
        cost_estimate=pl.CostEstimate(flops=flops, bytes_accessed=1 << 17, transcendentals=0),
        compiler_params=pltpu.CompilerParams(vmem_limit_bytes=(8 << 20) + extra),
    )


def sds(shape, dtype):
    return jax.ShapeDtypeStruct(shape, dtype)


def col_stats(x):
    mean = jnp.mean(x, axis=0, keepdims=True)
    cen = x - mean
    return mean, jnp.sum(cen * cen, axis=0, keepdims=True)


def tick_kernel(out_ref):
    out_ref[...] = jnp.zeros_like(out_ref)


def stats_kernel(own_ref, other_ref, gain_ref, bias_ref, b_in_ref, tick_ref, stat_ref, gb_ref):
    _, width = own_ref.shape
    rows = []
    for ref in (own_ref, other_ref):
        mean, m2 = col_stats(ref[...].astype(F32))
        rows += [mean, m2]
    stat_ref[...] = jnp.concatenate(rows, axis=0)
    gb_ref[0:1, :] = gain_ref[...].reshape(1, width)
    gb_ref[1:2, :] = bias_ref[...].reshape(1, width)
    gb_ref[2:3, :] = b_in_ref[...].reshape(1, width)


def merge_stats(parts, count):
    mean = parts[0][0]
    for p in parts[1:]:
        mean = mean + p[0]
    mean = mean * (1.0 / len(parts))
    m2 = None
    for p in parts:
        dev = p[0] - mean
        term = p[1] + count * (dev * dev)
        m2 = term if m2 is None else m2 + term
    return mean, m2


def half_stats(refs, half, count):
    at = 2 * half
    rows = [r[...] for r in refs]
    return merge_stats([(r[at : at + 1], r[at + 1 : at + 2]) for r in rows], count)


def merge_kernel(count, *refs):
    out = [row for half in (0, 1) for row in half_stats(refs[:-1], half, count)]
    refs[-1][...] = jnp.concatenate(out, axis=0)


def stack_kernel(*refs):
    rows = refs[0].shape[0]
    for i, r in enumerate(refs[:-1]):
        refs[-1][i * rows : (i + 1) * rows, :] = r[...]


def front_kernel(count, group_size, n_stat, *refs):
    stats, rest = refs[:n_stat], refs[n_stat:]
    own_ref, other_ref, gb_ref, gb2_ref, w_own_ref, w_other_ref, gain_ref, bias_ref, w_ref, stream_ref, out_ref = rest
    _, width = own_ref.shape
    full = 2 * width
    n_groups = width // group_size
    total = count * n_stat
    chan = lax.broadcasted_iota(jnp.int32, (n_groups, width), 1)
    grp = lax.broadcasted_iota(jnp.int32, (n_groups, width), 0) * group_size
    hot = jnp.where((chan >= grp) & (chan < grp + group_size), 1.0, 0.0)

    def over_group(row):
        per = jnp.sum(hot * row, axis=1, keepdims=True)
        return jnp.sum(hot * per, axis=0, keepdims=True)

    low = lax.axis_index("heads") == 0

    def in_order(own, other):
        return jnp.concatenate([jnp.where(low, own, other), jnp.where(low, other, own)], axis=1)

    normed = []
    for half, (x_ref, g_ref) in enumerate(((own_ref, gb_ref), (other_ref, gb2_ref))):
        mean, m2 = half_stats(stats, half, count)
        g_mean = over_group(mean) * (1.0 / group_size)
        dev = mean - g_mean
        var = over_group(m2 + total * (dev * dev)) * (1.0 / (total * group_size))
        scale = lax.rsqrt(var + 1e-06) * g_ref[0:1, :]
        normed.append((x_ref[...].astype(F32) - g_mean) * scale + g_ref[1:2, :])
    normed = in_order(*normed).astype(BF)
    x = []
    for wt_ref, g_ref in ((w_own_ref, gb_ref), (w_other_ref, gb2_ref)):
        x.append((jnp.dot(normed, wt_ref[...], preferred_element_type=F32) + g_ref[2:3, :]).astype(BF))
    stream_ref[...] = x[0]
    x = in_order(*[v.astype(F32) for v in x])
    x = x - jnp.sum(x, axis=1, keepdims=True) / full
    rstd = lax.rsqrt(jnp.sum(x * x, axis=1, keepdims=True) / full + 1e-05)
    row = (x * rstd * gain_ref[...].reshape(1, full) + bias_ref[...].reshape(1, full)).astype(BF)
    for i in range(3):
        out_ref[i] = jnp.dot(row, w_ref[i], preferred_element_type=F32).astype(BF)


def attn_kernel(sources, qkv_ref, *refs):
    n_src = max(s[0] for s in sources) + 1
    srcs, (w_ref, att_ref, send_ref) = refs[:n_src], refs[n_src:]
    tok, width = qkv_ref.shape[1:]

    def rows_of(which, c):
        parts = [qkv_ref[1 + which, :, c]] if sources[0][4] else []
        parts += [srcs[s[0]][s[1 + which] : s[1 + which] + s[3], c] for s in sources]
        return parts[0] if len(parts) == 1 else jnp.concatenate(parts, axis=0)

    pair = 2 * HD
    keys = sum(s[3] for s in sources) + (tok if sources[0][4] else 0)
    low = lax.broadcasted_iota(jnp.int32, (tok, pair), 1) < HD
    ones = jnp.ones((keys, pair), BF)
    cols = [slice(p * pair, (p + 1) * pair) for p in range(width // pair)]
    scores = []
    for c in cols:
        q = qkv_ref[0, :, c].astype(F32) * (HD ** (-0.5))
        q2 = jnp.concatenate([jnp.where(low, q, 0.0), jnp.where(low, 0.0, q)], axis=0).astype(BF)
        scores.append(lax.dot_general(q2, rows_of(0, c), (((1,), (1,)), ((), ())), preferred_element_type=F32))
    tops = [jnp.max(s, axis=1, keepdims=True) for s in scores]
    wts = [jnp.exp(s - m).astype(BF) for s, m in zip(scores, tops)]
    att = []
    for c, w in zip(cols, wts):
        both = jnp.dot(w, jnp.concatenate([rows_of(1, c), ones], axis=1), preferred_element_type=F32)
        out = both[:, :pair] / both[:, pair:]
        att.append(jnp.where(low, out[0:tok], out[tok:]).astype(BF))
    att = jnp.concatenate(att, axis=1)
    att_ref[...] = att
    first = pl.multiple_of((1 - lax.axis_index("heads")) * width, 128)
    send_ref[...] = jnp.dot(att, w_ref[:, pl.ds(first, width)], preferred_element_type=F32)


def own_kernel(att_ref, stream_ref, b_ref, w_ref, out_ref):
    width = stream_ref.shape[1]
    first = pl.multiple_of(lax.axis_index("heads") * width, 128)
    part = jnp.dot(att_ref[...], w_ref[:, pl.ds(first, width)], preferred_element_type=F32)
    out_ref[...] = part + stream_ref[...].astype(F32) + b_ref[...].reshape(1, width)


def body(hidden_in, gn_gain, gn_bias, w_in, b_in, ln_gain, ln_bias, w_qkv, stale_kv, w_out, b_out):
    tok, width = hidden_in.shape
    full = ln_gain.shape[0]
    group_size = full // GROUPS
    n = lax.axis_size("patch")
    swap = [(0, 1), (1, 0)]

    kv_own = stale_kv.reshape(2 * tok, width)
    partner = lambda k: [(i, i ^ k) for i in range(n)]

    def move(x, k):
        return lax.ppermute(x, "patch", partner(k)) if k else lax.ppermute(x, "heads", swap)

    direct = n == 8
    other = move(hidden_in, 0)
    tick = call(tick_kernel, sds((8, 128), F32), 0, flops=COVER)()
    stat_out = sds((STAT_ROWS, width), F32)
    local, gb = call(stats_kernel, (stat_out, sds((3, width), F32)), 6, flops=COVER)(
        hidden_in, other, gn_gain, gn_bias, b_in, tick
    )
    if direct:
        z2, z1 = move(kv_own, 4), move(kv_own, 2)
        z3 = move(kv_own, 6)
        strip_x = move(kv_own, 1)
        gb_other = move(gb, 0)
        w_other = move(w_in, 0)
        m0 = call(functools.partial(merge_kernel, float(1 * tok)), stat_out, 2, flops=COVER)(local, move(local, 1))
        m1 = call(functools.partial(merge_kernel, float(2 * tok)), stat_out, 2, flops=COVER)(m0, move(m0, 4))
        stats = [m1, move(m1, 2)]
        n0 = call(stack_kernel, sds((4 * tok, width), BF), 2)(z2, z1)
        f0 = move(n0, 1)
        f1 = move(z3, 1)
        strips = [strip_x, n0, f0, z3, f1]
        sources = [(0, 0, tok, tok, True), (1, 0 * tok, 1 * tok, tok, True), (1, 2 * tok, 3 * tok, tok, True), (2, 0 * tok, 1 * tok, tok, True), (2, 2 * tok, 3 * tok, tok, True), (3, 0, tok, tok, True), (4, 0, tok, tok, True)]
    else:
        gb_other = move(gb, 0)
        w_other = move(w_in, 0)
        rows = lax.all_gather(local, "patch")
        stats = [rows[i] for i in range(n)]

    count = float(tok * n) / len(stats)
    stream, qkv = call(
        functools.partial(front_kernel, count, group_size, len(stats)),
        (sds((tok, width), BF), sds((3, tok, width), BF)),
        len(stats) + 9,
        flops=COVER,
    )(*stats, hidden_in, other, gb, gb_other, w_in, w_other, ln_gain, ln_bias, w_qkv)
    n_keys = n * tok
    if not direct:
        kv_all = lax.all_gather(stale_kv, "patch", axis=1, tiled=True)
        kv_all = lax.dynamic_update_slice(kv_all, qkv[1:], (0, lax.axis_index("patch") * tok, 0))
        strips = [kv_all.reshape(2 * n_keys, width)]
        sources = [(0, 0, n_keys, n_keys, False)]
    attended, send = call(
        functools.partial(attn_kernel, sources),
        (sds((tok, width), BF), sds((tok, width), F32)),
        2 + len(strips),
        extra=64 * tok * n_keys + 4 * n_keys * width,
    )(qkv, *strips, w_out)
    received = move(send, 0)
    mine = call(own_kernel, sds((tok, width), F32), 4)(attended, stream, b_out, w_out)
    return mine + received


def solution(mesh):
    placed = (
        P(("groups", "patch"), "heads"),
        P("heads"),
        P("heads"),
        P(None, "heads"),
        P("heads"),
        P(),
        P(),
        P(None, None, "heads"),
        P(None, ("groups", "patch"), "heads"),
        P("heads", None),
        P("heads"),
    )

    return jax.shard_map(body, mesh=mesh, in_specs=placed, out_specs=P(("groups", "patch"), "heads"), check_vma=False)
```

```python
import functools

import jax
import jax.numpy as jnp
from jax import lax
from jax.experimental import pallas as pl
from jax.experimental.pallas import tpu as pltpu
from jax.sharding import PartitionSpec as P


HD = 64
GROUPS = 32
STAT_ROWS = 4
COVER = 10_000_000_000
VMEM = pltpu.VMEM
BF = jnp.bfloat16
F32 = jnp.float32


def call(kernel, out_shape, n_in, scratch=(), spaces=None, flops=0, extra=0):
    return pl.pallas_call(
        kernel,
        out_shape=out_shape,
        in_specs=[pl.BlockSpec(memory_space=(spaces or {}).get(i, VMEM)) for i in range(n_in)],
        out_specs=jax.tree.map(lambda _: pl.BlockSpec(memory_space=VMEM), out_shape),
        scratch_shapes=list(scratch),
        cost_estimate=pl.CostEstimate(flops=flops, bytes_accessed=1 << 17, transcendentals=0),
        compiler_params=pltpu.CompilerParams(vmem_limit_bytes=(8 << 20) + extra),
    )


def sds(shape, dtype):
    return jax.ShapeDtypeStruct(shape, dtype)


def col_stats(x):
    mean = jnp.mean(x, axis=0, keepdims=True)
    cen = x - mean
    return mean, jnp.sum(cen * cen, axis=0, keepdims=True)


def tick_kernel(out_ref):
    out_ref[...] = jnp.zeros_like(out_ref)


def stats_kernel(own_ref, other_ref, gain_ref, bias_ref, b_in_ref, tick_ref, stat_ref, gb_ref):
    _, width = own_ref.shape
    rows = []
    for ref in (own_ref, other_ref):
        mean, m2 = col_stats(ref[...].astype(F32))
        rows += [mean, m2]
    stat_ref[...] = jnp.concatenate(rows, axis=0)
    gb_ref[0:1, :] = gain_ref[...].reshape(1, width)
    gb_ref[1:2, :] = bias_ref[...].reshape(1, width)
    gb_ref[2:3, :] = b_in_ref[...].reshape(1, width)


def merge_stats(parts, count):
    mean = parts[0][0]
    for p in parts[1:]:
        mean = mean + p[0]
    mean = mean * (1.0 / len(parts))
    m2 = None
    for p in parts:
        dev = p[0] - mean
        term = p[1] + count * (dev * dev)
        m2 = term if m2 is None else m2 + term
    return mean, m2


def half_stats(refs, half, count):
    at = 2 * half
    rows = [r[...] for r in refs]
    return merge_stats([(r[at : at + 1], r[at + 1 : at + 2]) for r in rows], count)


def merge_kernel(count, *refs):
    out = [row for half in (0, 1) for row in half_stats(refs[:-1], half, count)]
    refs[-1][...] = jnp.concatenate(out, axis=0)


def stack_kernel(*refs):
    rows = refs[0].shape[0]
    for i, r in enumerate(refs[:-1]):
        refs[-1][i * rows : (i + 1) * rows, :] = r[...]


def group_sums(width, group_size):
    n_groups = width // group_size
    chan = lax.broadcasted_iota(jnp.int32, (n_groups, width), 1)
    grp = lax.broadcasted_iota(jnp.int32, (n_groups, width), 0) * group_size
    hot = jnp.where((chan >= grp) & (chan < grp + group_size), 1.0, 0.0)

    def over_group(row):
        per = jnp.sum(hot * row, axis=1, keepdims=True)
        return jnp.sum(hot * per, axis=0, keepdims=True)

    return over_group


def prep_kernel(count, group_size, stat_ref, own_ref, other_ref, ref_ref, x_ref):
    width = own_ref.shape[1]
    over_group = group_sums(width, group_size)
    out = []
    for half in (0, 1):
        mean, m2 = half_stats([stat_ref], half, count)
        g_mean = over_group(mean) * (1.0 / group_size)
        dev = mean - g_mean
        out += [g_mean, over_group(m2 + count * (dev * dev))]
    ref_ref[...] = jnp.concatenate(out, axis=0)
    low = lax.axis_index("heads") == 0
    own, other = own_ref[...].astype(F32), other_ref[...].astype(F32)
    x_ref[:, :width] = jnp.where(low, own, other)
    x_ref[:, width:] = jnp.where(low, other, own)


def front_kernel(count, group_size, n_stat, *refs):
    stats, rest = refs[:n_stat], refs[n_stat:]
    ref_ref, tok_ref, gb_ref, gb2_ref, w_own_ref, w_other_ref, gain_ref, bias_ref, w_ref, stream_ref, out_ref = rest
    full = tok_ref.shape[1]
    width = full // 2
    cells = count * group_size * (n_stat + 1)
    over_group = group_sums(width, group_size)
    low = lax.axis_index("heads") == 0

    def in_order(own, other):
        return jnp.concatenate([jnp.where(low, own, other), jnp.where(low, other, own)], axis=1)

    means, scales, shifts = [], [], []
    for half, g_ref in enumerate((gb_ref, gb2_ref)):
        at = 2 * half
        base, spread = ref_ref[at : at + 1, :], ref_ref[at + 1 : at + 2, :]
        mean_sum = mean_sq = None
        for s in stats:
            dev = s[at : at + 1, :] - base
            term = s[at + 1 : at + 2, :] + count * (dev * dev)
            mean_sum = dev if mean_sum is None else mean_sum + dev
            mean_sq = term if mean_sq is None else mean_sq + term
        off = over_group(mean_sum) * (1.0 / (group_size * (n_stat + 1)))
        var = (spread + over_group(mean_sq)) * (1.0 / cells) - off * off
        means.append(base + off)
        scales.append(lax.rsqrt(jnp.maximum(var, 0.0) + 1e-06) * g_ref[0:1, :])
        shifts.append(g_ref[1:2, :])
    normed = ((tok_ref[...] - in_order(*means)) * in_order(*scales) + in_order(*shifts)).astype(BF)
    x = []
    for wt_ref, g_ref in ((w_own_ref, gb_ref), (w_other_ref, gb2_ref)):
        x.append((jnp.dot(normed, wt_ref[...], preferred_element_type=F32) + g_ref[2:3, :]).astype(BF))
    stream_ref[...] = x[0]
    x = in_order(*[v.astype(F32) for v in x])
    x = x - jnp.sum(x, axis=1, keepdims=True) / full
    rstd = lax.rsqrt(jnp.sum(x * x, axis=1, keepdims=True) / full + 1e-05)
    row = (x * rstd * gain_ref[...].reshape(1, full) + bias_ref[...].reshape(1, full)).astype(BF)
    for i in range(3):
        out_ref[i] = jnp.dot(row, w_ref[i], preferred_element_type=F32).astype(BF)


def attn_kernel(sources, qkv_ref, *refs):
    n_src = max(s[0] for s in sources) + 1
    srcs, (w_ref, att_ref, send_ref) = refs[:n_src], refs[n_src:]
    tok, width = qkv_ref.shape[1:]

    def rows_of(which, c):
        parts = [qkv_ref[1 + which, :, c]] if sources[0][4] else []
        parts += [srcs[s[0]][s[1 + which] : s[1 + which] + s[3], c] for s in sources]
        return parts[0] if len(parts) == 1 else jnp.concatenate(parts, axis=0)

    pair = 2 * HD
    keys = sum(s[3] for s in sources) + (tok if sources[0][4] else 0)
    low = lax.broadcasted_iota(jnp.int32, (tok, pair), 1) < HD
    ones = jnp.ones((keys, pair), BF)
    cols = [slice(p * pair, (p + 1) * pair) for p in range(width // pair)]
    scores = []
    for c in cols:
        q = qkv_ref[0, :, c].astype(F32) * (HD ** (-0.5))
        q2 = jnp.concatenate([jnp.where(low, q, 0.0), jnp.where(low, 0.0, q)], axis=0).astype(BF)
        scores.append(lax.dot_general(q2, rows_of(0, c), (((1,), (1,)), ((), ())), preferred_element_type=F32))
    tops = [jnp.max(s, axis=1, keepdims=True) for s in scores]
    wts = [jnp.exp(s - m).astype(BF) for s, m in zip(scores, tops)]
    att = []
    for c, w in zip(cols, wts):
        both = jnp.dot(w, jnp.concatenate([rows_of(1, c), ones], axis=1), preferred_element_type=F32)
        out = both[:, :pair] / both[:, pair:]
        att.append(jnp.where(low, out[0:tok], out[tok:]).astype(BF))
    att = jnp.concatenate(att, axis=1)
    att_ref[...] = att
    first = pl.multiple_of((1 - lax.axis_index("heads")) * width, 128)
    send_ref[...] = jnp.dot(att, w_ref[:, pl.ds(first, width)], preferred_element_type=F32)


def own_kernel(att_ref, stream_ref, b_ref, w_ref, out_ref):
    width = stream_ref.shape[1]
    first = pl.multiple_of(lax.axis_index("heads") * width, 128)
    part = jnp.dot(att_ref[...], w_ref[:, pl.ds(first, width)], preferred_element_type=F32)
    out_ref[...] = part + stream_ref[...].astype(F32) + b_ref[...].reshape(1, width)


def body(hidden_in, gn_gain, gn_bias, w_in, b_in, ln_gain, ln_bias, w_qkv, stale_kv, w_out, b_out):
    tok, width = hidden_in.shape
    full = ln_gain.shape[0]
    group_size = full // GROUPS
    n = lax.axis_size("patch")
    swap = [(0, 1), (1, 0)]

    kv_own = stale_kv.reshape(2 * tok, width)
    partner = lambda k: [(i, i ^ k) for i in range(n)]

    def move(x, k):
        return lax.ppermute(x, "patch", partner(k)) if k else lax.ppermute(x, "heads", swap)

    direct = n == 8
    other = move(hidden_in, 0)
    tick = call(tick_kernel, sds((8, 128), F32), 0, flops=COVER)()
    stat_out = sds((STAT_ROWS, width), F32)
    local, gb = call(stats_kernel, (stat_out, sds((3, width), F32)), 6, flops=COVER)(
        hidden_in, other, gn_gain, gn_bias, b_in, tick
    )
    if direct:
        z2, z1 = move(kv_own, 4), move(kv_own, 2)
        z3 = move(kv_own, 6)
        strip_x = move(kv_own, 1)
        gb_other = move(gb, 0)
        w_other = move(w_in, 0)
        m0 = call(functools.partial(merge_kernel, float(1 * tok)), stat_out, 2, flops=COVER)(local, move(local, 1))
        m1 = call(functools.partial(merge_kernel, float(2 * tok)), stat_out, 2, flops=COVER)(m0, move(m0, 4))
        stats = [m1, move(m1, 2)]
        n0 = call(stack_kernel, sds((4 * tok, width), BF), 2)(z2, z1)
        f0 = move(n0, 1)
        f1 = move(z3, 1)
        strips = [strip_x, n0, f0, z3, f1]
        sources = [(0, 0, tok, tok, True), (1, 0 * tok, 1 * tok, tok, True), (1, 2 * tok, 3 * tok, tok, True), (2, 0 * tok, 1 * tok, tok, True), (2, 2 * tok, 3 * tok, tok, True), (3, 0, tok, tok, True), (4, 0, tok, tok, True)]
    else:
        gb_other = move(gb, 0)
        w_other = move(w_in, 0)
        rows = lax.all_gather(local, "patch")
        stats = [rows[i] for i in range(n)]

    count = float(tok * n) / len(stats)
    ref, x_full = call(
        functools.partial(prep_kernel, count, group_size), (stat_out, sds((tok, full), F32)), 3
    )(stats[0], hidden_in, other)
    stream, qkv = call(
        functools.partial(front_kernel, count, group_size, len(stats) - 1),
        (sds((tok, width), BF), sds((3, tok, width), BF)),
        len(stats) + 8,
        flops=COVER,
    )(*stats[1:], ref, x_full, gb, gb_other, w_in, w_other, ln_gain, ln_bias, w_qkv)
    n_keys = n * tok
    if not direct:
        kv_all = lax.all_gather(stale_kv, "patch", axis=1, tiled=True)
        kv_all = lax.dynamic_update_slice(kv_all, qkv[1:], (0, lax.axis_index("patch") * tok, 0))
        strips = [kv_all.reshape(2 * n_keys, width)]
        sources = [(0, 0, n_keys, n_keys, False)]
    attended, send = call(
        functools.partial(attn_kernel, sources),
        (sds((tok, width), BF), sds((tok, width), F32)),
        2 + len(strips),
        extra=64 * tok * n_keys + 4 * n_keys * width,
    )(qkv, *strips, w_out)
    received = move(send, 0)
    mine = call(own_kernel, sds((tok, width), F32), 4)(attended, stream, b_out, w_out)
    return mine + received


def solution(mesh):
    placed = (
        P(("groups", "patch"), "heads"),
        P("heads"),
        P("heads"),
        P(None, "heads"),
        P("heads"),
        P(),
        P(),
        P(None, None, "heads"),
        P(None, ("groups", "patch"), "heads"),
        P("heads", None),
        P("heads"),
    )

    return jax.shard_map(body, mesh=mesh, in_specs=placed, out_specs=P(("groups", "patch"), "heads"), check_vma=False)
```

```python
import functools

import jax
import jax.numpy as jnp
from jax import lax
from jax.experimental import pallas as pl
from jax.experimental.pallas import tpu as pltpu
from jax.sharding import PartitionSpec as P


HD = 64
GROUPS = 32
STAT_ROWS = 4
COVER = 10_000_000_000
VMEM = pltpu.VMEM
BF = jnp.bfloat16
F32 = jnp.float32


def call(kernel, out_shape, n_in, scratch=(), spaces=None, flops=0, extra=0):
    return pl.pallas_call(
        kernel,
        out_shape=out_shape,
        in_specs=[pl.BlockSpec(memory_space=(spaces or {}).get(i, VMEM)) for i in range(n_in)],
        out_specs=jax.tree.map(lambda _: pl.BlockSpec(memory_space=VMEM), out_shape),
        scratch_shapes=list(scratch),
        cost_estimate=pl.CostEstimate(flops=flops, bytes_accessed=1 << 17, transcendentals=0),
        compiler_params=pltpu.CompilerParams(vmem_limit_bytes=(8 << 20) + extra),
    )


def sds(shape, dtype):
    return jax.ShapeDtypeStruct(shape, dtype)


def col_stats(x):
    mean = jnp.mean(x, axis=0, keepdims=True)
    cen = x - mean
    return mean, jnp.sum(cen * cen, axis=0, keepdims=True)


def tick_kernel(out_ref):
    out_ref[...] = jnp.zeros_like(out_ref)


def stats_kernel(own_ref, other_ref, gain_ref, bias_ref, b_in_ref, tick_ref, stat_ref, gb_ref):
    _, width = own_ref.shape
    rows = []
    for ref in (own_ref, other_ref):
        mean, m2 = col_stats(ref[...].astype(F32))
        rows += [mean, m2]
    stat_ref[...] = jnp.concatenate(rows, axis=0)
    gb_ref[0:1, :] = gain_ref[...].reshape(1, width)
    gb_ref[1:2, :] = bias_ref[...].reshape(1, width)
    gb_ref[2:3, :] = b_in_ref[...].reshape(1, width)


def merge_stats(parts, count):
    mean = parts[0][0]
    for p in parts[1:]:
        mean = mean + p[0]
    mean = mean * (1.0 / len(parts))
    m2 = None
    for p in parts:
        dev = p[0] - mean
        term = p[1] + count * (dev * dev)
        m2 = term if m2 is None else m2 + term
    return mean, m2


def half_stats(refs, half, count):
    at = 2 * half
    rows = [r[...] for r in refs]
    return merge_stats([(r[at : at + 1], r[at + 1 : at + 2]) for r in rows], count)


def merge_kernel(count, *refs):
    out = [row for half in (0, 1) for row in half_stats(refs[:-1], half, count)]
    refs[-1][...] = jnp.concatenate(out, axis=0)


def stack_kernel(*refs):
    rows = refs[0].shape[0]
    for i, r in enumerate(refs[:-1]):
        refs[-1][i * rows : (i + 1) * rows, :] = r[...]


def group_sums(width, group_size):
    n_groups = width // group_size
    chan = lax.broadcasted_iota(jnp.int32, (n_groups, width), 1)
    grp = lax.broadcasted_iota(jnp.int32, (n_groups, width), 0) * group_size
    hot = jnp.where((chan >= grp) & (chan < grp + group_size), 1.0, 0.0)

    def over_group(row):
        per = jnp.sum(hot * row, axis=1, keepdims=True)
        return jnp.sum(hot * per, axis=0, keepdims=True)

    return over_group


def prep_kernel(count, group_size, stat_ref, own_ref, other_ref, ref_ref, x_ref):
    width = own_ref.shape[1]
    over_group = group_sums(width, group_size)
    out = []
    for half in (0, 1):
        mean, m2 = half_stats([stat_ref], half, count)
        g_mean = over_group(mean) * (1.0 / group_size)
        dev = mean - g_mean
        out += [g_mean, over_group(m2 + count * (dev * dev))]
    ref_ref[...] = jnp.concatenate(out, axis=0)
    low = lax.axis_index("heads") == 0
    own, other = own_ref[...].astype(F32), other_ref[...].astype(F32)
    x_ref[:, :width] = jnp.where(low, own, other)
    x_ref[:, width:] = jnp.where(low, other, own)


def front_kernel(count, group_size, n_stat, *refs):
    stats, rest = refs[:n_stat], refs[n_stat:]
    ref_ref, tok_ref, gb_ref, gb2_ref, w_own_ref, w_other_ref, gain_ref, bias_ref, w_ref, stream_ref, out_ref = rest
    full = tok_ref.shape[1]
    width = full // 2
    cells = count * group_size * (n_stat + 1)
    over_group = group_sums(width, group_size)
    low = lax.axis_index("heads") == 0

    def in_order(own, other):
        return jnp.concatenate([jnp.where(low, own, other), jnp.where(low, other, own)], axis=1)

    means, scales, shifts = [], [], []
    for half, g_ref in enumerate((gb_ref, gb2_ref)):
        at = 2 * half
        base, spread = ref_ref[at : at + 1, :], ref_ref[at + 1 : at + 2, :]
        mean_sum = mean_sq = None
        for s in stats:
            dev = s[at : at + 1, :] - base
            term = s[at + 1 : at + 2, :] + count * (dev * dev)
            mean_sum = dev if mean_sum is None else mean_sum + dev
            mean_sq = term if mean_sq is None else mean_sq + term
        off = over_group(mean_sum) * (1.0 / (group_size * (n_stat + 1)))
        var = (spread + over_group(mean_sq)) * (1.0 / cells) - off * off
        means.append(base + off)
        scales.append(lax.rsqrt(jnp.maximum(var, 0.0) + 1e-06) * g_ref[0:1, :])
        shifts.append(g_ref[1:2, :])
    normed = ((tok_ref[...] - in_order(*means)) * in_order(*scales) + in_order(*shifts)).astype(BF)
    x = []
    for wt_ref, g_ref in ((w_own_ref, gb_ref), (w_other_ref, gb2_ref)):
        x.append((jnp.dot(normed, wt_ref[...], preferred_element_type=F32) + g_ref[2:3, :]).astype(BF))
    stream_ref[...] = x[0]
    x = in_order(*[v.astype(F32) for v in x])
    x = x - jnp.sum(x, axis=1, keepdims=True) / full
    rstd = lax.rsqrt(jnp.sum(x * x, axis=1, keepdims=True) / full + 1e-05)
    row = (x * rstd * gain_ref[...].reshape(1, full) + bias_ref[...].reshape(1, full)).astype(BF)
    for i in range(3):
        out_ref[i] = jnp.dot(row, w_ref[i], preferred_element_type=F32).astype(BF)


def attn_kernel(sources, qkv_ref, *refs):
    n_src = max(s[0] for s in sources) + 1
    srcs, (w_ref, att_ref, send_ref) = refs[:n_src], refs[n_src:]
    tok, width = qkv_ref.shape[1:]

    def rows_of(which, c):
        parts = [qkv_ref[1 + which, :, c]] if sources[0][4] else []
        parts += [srcs[s[0]][s[1 + which] : s[1 + which] + s[3], c] for s in sources]
        return parts[0] if len(parts) == 1 else jnp.concatenate(parts, axis=0)

    pair = 2 * HD
    keys = sum(s[3] for s in sources) + (tok if sources[0][4] else 0)
    low = lax.broadcasted_iota(jnp.int32, (tok, pair), 1) < HD
    ones = jnp.ones((keys, pair), BF)
    cols = [slice(p * pair, (p + 1) * pair) for p in range(width // pair)]
    scores = []
    for c in cols:
        q = qkv_ref[0, :, c].astype(F32) * (HD ** (-0.5))
        q2 = jnp.concatenate([jnp.where(low, q, 0.0), jnp.where(low, 0.0, q)], axis=0).astype(BF)
        scores.append(lax.dot_general(q2, rows_of(0, c), (((1,), (1,)), ((), ())), preferred_element_type=F32))
    tops = [jnp.max(s, axis=1, keepdims=True) for s in scores]
    wts = [jnp.exp(s - m).astype(BF) for s, m in zip(scores, tops)]
    att = []
    for c, w in zip(cols, wts):
        both = jnp.dot(w, jnp.concatenate([rows_of(1, c), ones], axis=1), preferred_element_type=F32)
        out = both[:, :pair] / both[:, pair:]
        att.append(jnp.where(low, out[0:tok], out[tok:]).astype(BF))
    att = jnp.concatenate(att, axis=1)
    att_ref[...] = att
    first = pl.multiple_of((1 - lax.axis_index("heads")) * width, 128)
    send_ref[...] = jnp.dot(att, w_ref[:, pl.ds(first, width)], preferred_element_type=F32).astype(BF)


def own_kernel(att_ref, stream_ref, b_ref, w_ref, out_ref):
    width = stream_ref.shape[1]
    first = pl.multiple_of(lax.axis_index("heads") * width, 128)
    part = jnp.dot(att_ref[...], w_ref[:, pl.ds(first, width)], preferred_element_type=F32)
    out_ref[...] = part + stream_ref[...].astype(F32) + b_ref[...].reshape(1, width)


def body(hidden_in, gn_gain, gn_bias, w_in, b_in, ln_gain, ln_bias, w_qkv, stale_kv, w_out, b_out):
    tok, width = hidden_in.shape
    full = ln_gain.shape[0]
    group_size = full // GROUPS
    n = lax.axis_size("patch")
    swap = [(0, 1), (1, 0)]

    kv_own = stale_kv.reshape(2 * tok, width)
    partner = lambda k: [(i, i ^ k) for i in range(n)]

    def move(x, k):
        return lax.ppermute(x, "patch", partner(k)) if k else lax.ppermute(x, "heads", swap)

    direct = n == 8
    other = move(hidden_in, 0)
    tick = call(tick_kernel, sds((8, 128), F32), 0, flops=COVER)()
    stat_out = sds((STAT_ROWS, width), F32)
    local, gb = call(stats_kernel, (stat_out, sds((3, width), F32)), 6, flops=COVER)(
        hidden_in, other, gn_gain, gn_bias, b_in, tick
    )
    if direct:
        z2, z1 = move(kv_own, 4), move(kv_own, 2)
        z3 = move(kv_own, 6)
        strip_x = move(kv_own, 1)
        gb_other = move(gb, 0)
        w_other = move(w_in, 0)
        m0 = call(functools.partial(merge_kernel, float(1 * tok)), stat_out, 2, flops=COVER)(local, move(local, 1))
        m1 = call(functools.partial(merge_kernel, float(2 * tok)), stat_out, 2, flops=COVER)(m0, move(m0, 4))
        stats = [m1, move(m1, 2)]
        n0 = call(stack_kernel, sds((4 * tok, width), BF), 2)(z2, z1)
        f0 = move(n0, 1)
        f1 = move(z3, 1)
        strips = [strip_x, n0, f0, z3, f1]
        sources = [(0, 0, tok, tok, True), (1, 0 * tok, 1 * tok, tok, True), (1, 2 * tok, 3 * tok, tok, True), (2, 0 * tok, 1 * tok, tok, True), (2, 2 * tok, 3 * tok, tok, True), (3, 0, tok, tok, True), (4, 0, tok, tok, True)]
    else:
        gb_other = move(gb, 0)
        w_other = move(w_in, 0)
        rows = lax.all_gather(local, "patch")
        stats = [rows[i] for i in range(n)]

    count = float(tok * n) / len(stats)
    ref, x_full = call(
        functools.partial(prep_kernel, count, group_size), (stat_out, sds((tok, full), F32)), 3
    )(stats[0], hidden_in, other)
    stream, qkv = call(
        functools.partial(front_kernel, count, group_size, len(stats) - 1),
        (sds((tok, width), BF), sds((3, tok, width), BF)),
        len(stats) + 8,
        flops=COVER,
    )(*stats[1:], ref, x_full, gb, gb_other, w_in, w_other, ln_gain, ln_bias, w_qkv)
    n_keys = n * tok
    if not direct:
        kv_all = lax.all_gather(stale_kv, "patch", axis=1, tiled=True)
        kv_all = lax.dynamic_update_slice(kv_all, qkv[1:], (0, lax.axis_index("patch") * tok, 0))
        strips = [kv_all.reshape(2 * n_keys, width)]
        sources = [(0, 0, n_keys, n_keys, False)]
    attended, send = call(
        functools.partial(attn_kernel, sources),
        (sds((tok, width), BF), sds((tok, width), BF)),
        2 + len(strips),
        extra=64 * tok * n_keys + 4 * n_keys * width,
    )(qkv, *strips, w_out)
    received = move(send, 0)
    mine = call(own_kernel, sds((tok, width), F32), 4)(attended, stream, b_out, w_out)
    return mine + received.astype(F32)


def solution(mesh):
    placed = (
        P(("groups", "patch"), "heads"),
        P("heads"),
        P("heads"),
        P(None, "heads"),
        P("heads"),
        P(),
        P(),
        P(None, None, "heads"),
        P(None, ("groups", "patch"), "heads"),
        P("heads", None),
        P("heads"),
    )

    return jax.shard_map(body, mesh=mesh, in_specs=placed, out_specs=P(("groups", "patch"), "heads"), check_vma=False)
```
